32 devices in a mesh: groups: 2 (over x), dp: 8 (over z, y), head: 2 (over core).
Axes of the slice: x: 2, y: 2, z: 4, core: 2. Of those that a mesh axis runs over, the one named last changes fastest.
Arguments:
- queries: bfloat16 [96, 128, 576], P(('groups', 'dp'), 'head'), parts along dimension 0, as said below
- latent_key_cache: bfloat16 [96, 192, 576], P(('groups', 'dp')), parts along dimension 0, as said below
- lengths: int32 [96], P(('groups', 'dp')), parts along dimension 0, may hold values from 48 to 192, as said below
- counts: int32 [16], P('groups'), parts along dimension 0, may hold values from 1 to 6, as said below
- residual: bfloat16 [96, 7168], P(('groups', 'dp', 'head')), parts along dimension 0
- value_up_weight: bfloat16 [2, 64, 512, 128], P('head', 'dp'), may hold values from -0.25 to 0.25
- output_proj: bfloat16 [2, 8192, 7168], P('head', 'dp'), may hold values from -0.125 to 0.125
- norm_gain: float32 [7168], replicated, may hold values from 0.1 to 1.9
- gate_weight: bfloat16 [7168, 9216], P(None, ('dp', 'head')), may hold values from -0.0625 to 0.0625
- up_weight: bfloat16 [7168, 9216], P(None, ('dp', 'head')), may hold values from -0.0625 to 0.0625
- down_weight: bfloat16 [9216, 7168], P(('dp', 'head')), may hold values from -0.125 to 0.125
Outputs:
- layer_out: bfloat16 [96, 7168], P(('groups', 'dp', 'head')), parts along dimension 0
The draws below stay inside these ranges and needn't reach their ends.
There are 2 independent parts, one for each index of `groups`. The reference program is written for one: setup_inputs(seed, part) draws one part's arguments, and reference() takes and returns one part's arrays. A program takes and returns all parts, laid end to end along the dimension named above; an argument that names none is the same for every part. Nothing has to cross between parts.
Inputs may be any that keep to these rules, and one draw needn't show every extreme that they name: Rank r's live rows are its first counts[r] slots; in every draw some rank has all 6 slots live. `lengths`: in every draw some live row has a cache of exactly 192 positions. real-valued latent queries of order one, larger where a query follows a cached key. `latent_key_cache`: real-valued latent keys of order one.
All inputs are finite; a program needn't handle non-finite values.
Results may differ from the reference program's by a relative error of at most 0.006.
Values may be sent and summed in bfloat16 or wider, within the bound.
No kernel may reach another device: no remote copies, remote signals or barrier semaphores. Data moves between devices by JAX's collectives and lax.ppermute only.
A program may use at most 128 MiB of HBM per device.

```python
import math
import jax
import jax.numpy as jnp
from jax import lax

D = 7168
HEAD_COUNT = 128
HEAD_VALUE_WIDTH = 128
LATENT_WIDTH = 512
ROTARY_WIDTH = 64
FF = 9216
SLOTS = 6
LMAX = 192
ROWS = 48
N_DP = 8
N_HEAD = 2


def attention_inputs(key):
    cache_key = jax.random.fold_in(key, 101)
    query_key = jax.random.fold_in(key, 102)
    latent_width = LATENT_WIDTH + ROTARY_WIDTH
    cache_draw = jnp.clip(jax.random.normal(cache_key, (ROWS, LMAX, latent_width), jnp.float32), -6.0, 6.0)
    query_draw = jnp.clip(jax.random.normal(query_key, (ROWS, HEAD_COUNT, latent_width), jnp.float32), -6.0, 6.0)
    return (cache_draw, query_draw)


def draw_queries(key, part):
    return attention_inputs(key)[1].astype(jnp.bfloat16)


def draw_latent_key_cache(key, part):
    return attention_inputs(key)[0].astype(jnp.bfloat16)


def draw_residual(key, part):
    spread = math.log(10.0)
    row_scale = jnp.exp(jax.random.uniform(jax.random.fold_in(key, 201), (ROWS, 1), jnp.float32, 0.0, spread)) / 3.1622777
    column_scale = jnp.exp(jax.random.uniform(jax.random.fold_in(key, 202), (1, D), jnp.float32, 0.0, spread)) / 3.1622777
    base_key = jax.random.fold_in(key, 203)
    base_draw = jnp.clip(jax.random.normal(base_key, (ROWS, D), jnp.float32), -6.0, 6.0)
    return (base_draw * row_scale * column_scale).astype(jnp.bfloat16)


def draw_counts(key, part):
    base_draw = jax.random.randint(jax.random.fold_in(key, 301), (N_DP,), 1, SLOTS + 1)
    full_rank = jax.random.randint(jax.random.fold_in(key, 302), (), 0, N_DP)
    return jnp.where(jnp.arange(N_DP, dtype=jnp.int32) == full_rank, SLOTS, base_draw).astype(jnp.int32)


def draw_lengths(key, part):
    shortest = LMAX // 4
    rank_caps = jax.random.randint(jax.random.fold_in(key, 401), (N_DP, 1), shortest, LMAX + 1)
    row_lengths = jax.random.randint(jax.random.fold_in(key, 402), (N_DP, SLOTS), shortest, rank_caps + 1)
    long_rank = jax.random.randint(jax.random.fold_in(key, 403), (), 0, N_DP)
    chosen = (jnp.arange(N_DP, dtype=jnp.int32)[:, None] == long_rank) & (jnp.arange(SLOTS, dtype=jnp.int32)[None, :] == 0)
    row_lengths = jnp.where(chosen, LMAX, row_lengths)
    return row_lengths.reshape(ROWS).astype(jnp.int32)


def shard_levels(key, dims, pieces, least, top_value):
    def one(position, parts):
        steps = jax.random.uniform(jax.random.fold_in(jax.random.fold_in(key, 6), position), (parts,), jnp.float32, least / len(pieces), top_value / len(pieces))
        return jnp.repeat(jnp.exp(steps), dims[position] // parts).reshape((-1,) + (1,) * (len(dims) - position - 1))

    factor_of = one(*pieces[0])
    for cut in pieces[1:]:
        factor_of = factor_of * one(*cut)
    return factor_of


def gaussian(key, shape, width, reach, split=(), kind=jnp.bfloat16):
    drawn = width * jax.random.normal(key, shape, jnp.float32)
    if split:
        drawn = drawn * shard_levels(key, shape, split, -0.22, 0.18)
    return jnp.clip(drawn, -reach, reach).astype(kind)


def setup_inputs(seed: int = 0, part: int = 0) -> dict:
    key_list = jax.random.split(jax.random.key(seed), 12)
    part_keys = jax.random.split(jax.random.fold_in(key_list[11], part), 12)
    queries = draw_queries(jax.random.fold_in(jax.random.fold_in(key_list[11], part), 71), part)
    latent_key_cache = draw_latent_key_cache(jax.random.fold_in(jax.random.fold_in(key_list[11], part), 71), part)
    lengths = draw_lengths(jax.random.fold_in(jax.random.fold_in(key_list[11], part), 71), part)
    counts = draw_counts(jax.random.fold_in(jax.random.fold_in(key_list[11], part), 71), part)
    residual = draw_residual(jax.random.fold_in(jax.random.fold_in(key_list[11], part), 71), part)
    value_up_weight = gaussian(key_list[5], (N_HEAD, HEAD_COUNT // N_HEAD, LATENT_WIDTH, HEAD_VALUE_WIDTH), LATENT_WIDTH ** -0.5, 0.25, ((0, 2), (1, 8)))
    output_proj = gaussian(key_list[6], (N_HEAD, HEAD_COUNT // N_HEAD * HEAD_VALUE_WIDTH, D), (HEAD_COUNT * HEAD_VALUE_WIDTH // 8) ** -0.5, 0.125, ((0, 2), (1, 8)))
    norm_gain = jnp.clip(1.0 + 0.18 * jax.random.normal(key_list[7], (D,), jnp.float32), 0.1, 1.9)
    gate_weight = gaussian(key_list[8], (D, FF), D ** -0.5, 0.0625, ((1, 16),))
    up_weight = gaussian(key_list[9], (D, FF), D ** -0.5, 0.0625, ((1, 16),))
    down_weight = gaussian(key_list[10], (FF, D), (FF // 4) ** -0.5, 0.125, ((0, 16),))
    return dict(queries=queries, latent_key_cache=latent_key_cache, lengths=lengths, counts=counts, residual=residual, value_up_weight=value_up_weight, output_proj=output_proj, norm_gain=norm_gain, gate_weight=gate_weight, up_weight=up_weight, down_weight=down_weight)


score_scale = 0.07216878364870322
norm_epsilon = 1e-06
masked_score = -1e+30

def reference(queries, latent_key_cache, lengths, counts, residual, value_up_weight, output_proj, norm_gain, gate_weight, up_weight, down_weight):
    row_total = queries.shape[0]
    positions = jnp.arange(LMAX, dtype=jnp.int32)
    valid_keys = positions[None, :] < lengths[:, None]
    scores = jnp.einsum('rhc,rjc->rhj', queries.astype(jnp.float32), latent_key_cache.astype(jnp.float32)) * score_scale
    scores = jnp.where(valid_keys[:, None, :], scores, masked_score)
    row_top = lax.optimization_barrier(jnp.max(scores, axis=-1, keepdims=True))
    probs_full = jnp.exp(scores - row_top)
    softmax_denominator = lax.optimization_barrier(jnp.sum(probs_full, axis=-1))
    attention_weights = probs_full.astype(jnp.bfloat16)
    weighted_latent = jnp.einsum('ukw,uwm->ukm', attention_weights.astype(jnp.float32), latent_key_cache[:, :, :LATENT_WIDTH].astype(jnp.float32)) / softmax_denominator[:, :, None]
    row_ids = jnp.arange(row_total, dtype=jnp.int32)
    live_rows = row_ids % SLOTS < counts[row_ids // SLOTS]
    latent_out = jnp.where(live_rows[:, None, None], weighted_latent, 0.0).astype(jnp.bfloat16)
    per_head_maps = value_up_weight.reshape(HEAD_COUNT, LATENT_WIDTH, HEAD_VALUE_WIDTH).astype(jnp.float32)
    values = jnp.einsum('rhc,hcd->rhd', latent_out.astype(jnp.float32), per_head_maps).astype(jnp.bfloat16)
    attention = jnp.dot(values.reshape(row_total, HEAD_COUNT * HEAD_VALUE_WIDTH), output_proj.reshape(HEAD_COUNT * HEAD_VALUE_WIDTH, D), preferred_element_type=jnp.float32)
    layer_state = residual.astype(jnp.float32) + attention
    mean_square = lax.optimization_barrier(jnp.mean(layer_state * layer_state, axis=-1, keepdims=True))
    normed = (layer_state * lax.rsqrt(mean_square + norm_epsilon) * norm_gain).astype(jnp.bfloat16)
    gate_part = jnp.dot(normed, gate_weight, preferred_element_type=jnp.float32)
    up_part = jnp.dot(normed, up_weight, preferred_element_type=jnp.float32)
    hidden_units = (jax.nn.silu(gate_part) * up_part).astype(jnp.bfloat16)
    feed_forward = jnp.dot(hidden_units, down_weight, preferred_element_type=jnp.float32)
    return jnp.where(live_rows[:, None], layer_state + feed_forward, 0.0).astype(jnp.bfloat16)
```

```python
import jax
import jax.numpy as jnp
from jax import lax
from jax.sharding import PartitionSpec as P

LATENT_WIDTH = 512
LANES = 128

score_scale = 0.07216878364870322
norm_epsilon = 1e-06
masked_score = -1e30
f32 = jnp.float32
bf16 = jnp.bfloat16


def on_device(n_dp, queries, latent_key_cache, lengths, counts, residual, value_up_weight,
              output_proj, norm_gain, gate_weight, up_weight, down_weight):
    slots = queries.shape[0]
    heads = queries.shape[1]
    cache_length = latent_key_cache.shape[1]
    owner_rows, width = residual.shape
    tiles = width // LANES
    me = lax.axis_index("dp")
    my_head = lax.axis_index("head")

    def to_peer(x, k):
        return lax.ppermute(x, "dp", [(i, i ^ k) for i in range(n_dp)])

    def to_twin(x):
        return lax.ppermute(x, "head", [(0, 1), (1, 0)])

    def reduce_rows(part):
        mine = part[0] + to_twin(part[1].astype(bf16)).astype(f32)
        sent = mine.astype(bf16)
        total = mine[0]
        for k in range(1, n_dp):
            total = total + to_peer(sent[k], k).astype(f32)
        return total

    live_count = jnp.sum(jnp.where(jnp.arange(n_dp, dtype=jnp.int32) == me, counts, 0))
    live_slots = jnp.arange(slots, dtype=jnp.int32) < live_count
    scores = jnp.einsum("rhc,rjc->rhj", queries, latent_key_cache, preferred_element_type=f32) * score_scale
    positions = jnp.arange(cache_length, dtype=jnp.int32)
    valid = positions[None, :] < lengths[:, None]
    scores = jnp.where(valid[:, None, :], scores, masked_score)
    row_top = jnp.max(scores, axis=-1, keepdims=True)
    probs = jnp.exp(scores - row_top)
    denominator = jnp.sum(probs, axis=-1)
    weighted = jnp.einsum("ukw,uwm->ukm", probs.astype(bf16), latent_key_cache[:, :, :LATENT_WIDTH],
                          preferred_element_type=f32)
    latent = jnp.where(live_slots[:, None, None], weighted / denominator[:, :, None], 0.0).astype(bf16)
    per_rank = heads // n_dp
    latent = latent.reshape(slots, n_dp, per_rank, LATENT_WIDTH)
    blocks = []
    for k in range(n_dp):
        piece = lax.dynamic_index_in_dim(latent, me ^ k, 1, keepdims=False)
        blocks.append(to_peer(piece, k) if k else piece)
    arrived = jnp.stack(blocks)
    arrived = arrived.reshape(n_dp, 2, owner_rows, per_rank, LATENT_WIDTH)
    arrived = jnp.swapaxes(arrived, 0, 1)
    arrived = jnp.where(my_head == 0, arrived, arrived[::-1])
    arrived = arrived.reshape(n_dp * slots, per_rank, LATENT_WIDTH)
    values = jnp.einsum("rhc,hcd->rhd", arrived, value_up_weight[0], preferred_element_type=f32).astype(bf16)
    values = values.reshape(n_dp * slots, -1)
    part = jnp.dot(values, output_proj[0], preferred_element_type=f32)
    attention = reduce_rows(part.reshape(2, n_dp, owner_rows * tiles, LANES))
    attention = attention.reshape(owner_rows, tiles, LANES)
    state = residual.astype(f32).reshape(owner_rows, tiles, LANES) + attention
    mean_square = jnp.sum(state * state, axis=(1, 2), keepdims=True) / width
    normed = (state * lax.rsqrt(mean_square + norm_epsilon) * norm_gain.reshape(tiles, LANES)).astype(bf16)
    normed = normed.reshape(owner_rows * tiles, LANES)
    rows = jnp.stack([normed] + [to_peer(normed, k) for k in range(1, n_dp)])
    rows = jnp.stack([rows, to_twin(rows)])
    rows = rows.reshape(n_dp * slots, width)
    gate_part = jnp.dot(rows, gate_weight, preferred_element_type=f32)
    up_part = jnp.dot(rows, up_weight, preferred_element_type=f32)
    hidden = (jax.nn.silu(gate_part) * up_part).astype(bf16)
    part = jnp.dot(hidden, down_weight, preferred_element_type=f32)
    feed_forward = reduce_rows(part.reshape(2, n_dp, owner_rows * tiles, LANES))
    out = state + feed_forward.reshape(owner_rows, tiles, LANES)
    owner_live = my_head * owner_rows + jnp.arange(owner_rows, dtype=jnp.int32) < live_count
    return jnp.where(owner_live[:, None, None], out, 0.0).astype(bf16).reshape(owner_rows, width)


def solution(mesh):
    n_dp = mesh.shape["dp"]
    in_specs = (
        P(("groups", "dp"), "head", None),
        P(("groups", "dp"), None, None),
        P(("groups", "dp")),
        P("groups"),
        P(("groups", "dp", "head"), None),
        P("head", "dp", None, None),
        P("head", "dp", None),
        P(),
        P(None, ("dp", "head")),
        P(None, ("dp", "head")),
        P(("dp", "head"), None),
    )
    out_specs = P(("groups", "dp", "head"), None)

    def step(*args):
        return on_device(n_dp, *args)

    return jax.shard_map(step, mesh=mesh, in_specs=in_specs, out_specs=out_specs, check_vma=False)
```

```python
import functools

import jax
import jax.numpy as jnp
from jax import lax
from jax.experimental import pallas as pl
from jax.experimental.pallas import tpu as pltpu
from jax.sharding import PartitionSpec as P

LATENT_WIDTH = 512
PARTS = 4

score_scale = 0.07216878364870322
norm_epsilon = 1e-06
masked_score = -1e30
f32 = jnp.float32
bf16 = jnp.bfloat16
VMEM = pltpu.VMEM
MIB = 1 << 20


def in_hbm(arrays):
    return [pltpu.with_memory_space_constraint(x, pltpu.HBM) for x in arrays]


def vmem(n):
    return [pl.BlockSpec(memory_space=VMEM)] * n


def params(mib):
    return pltpu.CompilerParams(vmem_limit_bytes=mib * MIB)


def load_kernel(count, pieces, *refs):
    sources, targets, sems = refs[1 : 1 + count], refs[1 + count : 1 + 2 * count], refs[1 + 2 * count]
    copies = row_copies(sources, targets, sems, pieces)
    for copy in copies:
        copy.start()
    for copy in copies:
        copy.wait()


def row_copies(sources, targets, sems, pieces):
    copies = []
    for n, (source, target) in enumerate(zip(sources, targets)):
        count = pieces if source.shape[0] % (16 * pieces) == 0 else 1
        step = source.shape[0] // count
        for p in range(count):
            at = pl.ds(p * step, step)
            copies.append(pltpu.make_async_copy(source.at[at], target.at[at], sems.at[n, p]))
    return copies


def load(after, weights, mib):
    pieces = 4
    size = sum(w.size for w in weights) * 2
    return pl.pallas_call(
        functools.partial(load_kernel, len(weights), pieces),
        out_shape=[jax.ShapeDtypeStruct(w.shape, w.dtype) for w in weights],
        in_specs=[pl.BlockSpec(memory_space=pl.ANY)] * (1 + len(weights)),
        out_specs=vmem(len(weights)),
        scratch_shapes=[pltpu.SemaphoreType.DMA((len(weights), pieces))],
        compiler_params=params(mib),
        cost_estimate=pl.CostEstimate(flops=0, bytes_accessed=2 * size, transcendentals=0),
        name="load",
    )(after, *in_hbm(weights))


def row_ids(rows, columns, slots):
    i = lax.broadcasted_iota(jnp.int32, (rows, columns), 0).astype(f32)
    unit = float(slots * PARTS)
    block = jnp.floor((i + 0.5) / unit)
    inner = i - block * unit
    part = jnp.floor((inner + 0.5) / slots)
    return part, block * slots + (inner - part * slots)


def attention_kernel(n_dp, counts_hbm, lengths_hbm, q_hbm, cache_hbm, *refs):
    n_weights = 2
    weights, outs = refs[:n_weights], refs[n_weights : n_weights + n_dp]
    loaded = refs[n_weights + n_dp : 2 * n_weights + n_dp]
    counts_ref, lengths_ref, q_ref, cache_ref, held, sems, scalar_sems, weight_sems = refs[2 * n_weights + n_dp :]
    fetches = row_copies(weights, loaded, weight_sems, weight_sems.shape[1])
    slots = q_ref.shape[0]
    scalars = [
        pltpu.make_async_copy(counts_hbm, counts_ref, scalar_sems.at[0]),
        pltpu.make_async_copy(lengths_hbm, lengths_ref, scalar_sems.at[1]),
    ]
    copies = []
    for row in range(slots):
        copies.append(
            (
                pltpu.make_async_copy(q_hbm.at[row], q_ref.at[row], sems.at[0, row]),
                pltpu.make_async_copy(cache_hbm.at[row], cache_ref.at[row], sems.at[1, row]),
            )
        )
    for copy in scalars + [c for pair in copies for c in pair]:
        copy.start()
    for copy in fetches:
        copy.start()
    for copy in scalars:
        copy.wait()
    me = lax.axis_index("dp")
    for row in range(slots):
        for copy in copies[row]:
            copy.wait()
        q = q_ref[row]
        cache = cache_ref[row]
        scores = lax.dot_general(q, cache, (((1,), (1,)), ((), ())), preferred_element_type=f32) * score_scale
        position = lax.broadcasted_iota(jnp.int32, scores.shape, 1)
        scores = jnp.where(position < lengths_ref[row], scores, masked_score)
        probs = jnp.exp(scores - jnp.max(scores, axis=-1, keepdims=True))
        denominator = jnp.sum(probs, axis=-1, keepdims=True)
        weighted = jnp.dot(probs.astype(bf16), cache[:, :LATENT_WIDTH], preferred_element_type=f32)
        latent = jnp.where(row < counts_ref[me], weighted / denominator, 0.0).astype(bf16)
        held[row] = latent.reshape(held.shape[1:])
    for k in range(n_dp):
        for row in range(slots):
            outs[k][row] = held[row, me ^ k]
    for copy in fetches:
        copy.wait()


def attend(n_dp, counts, lengths, queries, cache, weights):
    slots, heads, _ = queries.shape
    per_rank = heads // n_dp
    block = jax.ShapeDtypeStruct((slots, per_rank, LATENT_WIDTH), bf16)
    return pl.pallas_call(
        functools.partial(attention_kernel, n_dp),
        out_shape=[block] * n_dp + [jax.ShapeDtypeStruct(w.shape, w.dtype) for w in weights],
        in_specs=[pl.BlockSpec(memory_space=pl.ANY)] * (4 + len(weights)),
        out_specs=vmem(n_dp + len(weights)),
        scratch_shapes=[
            pltpu.SMEM(counts.shape, jnp.int32),
            pltpu.SMEM(lengths.shape, jnp.int32),
            VMEM(queries.shape, bf16),
            VMEM(cache.shape, bf16),
            VMEM((slots, n_dp, per_rank, LATENT_WIDTH), bf16),
            pltpu.SemaphoreType.DMA((2, slots)),
            pltpu.SemaphoreType.DMA((2,)),
            pltpu.SemaphoreType.DMA((len(weights), 2)),
        ],
        compiler_params=params(8),
        name="attend",
    )(*in_hbm([counts, lengths, queries, cache, *weights]))


def spread(rows, slots):
    wide_rows = rows * PARTS
    _, source = row_ids(wide_rows, rows, slots)
    column = lax.broadcasted_iota(jnp.int32, (wide_rows, rows), 1).astype(f32)
    return (source == column).astype(bf16)


def expand(x, slots):
    return jnp.dot(spread(x.shape[0], slots), x, preferred_element_type=f32).astype(bf16)


def write_units(wide_ref, weight_ref, acc_ref, keep_ref, give_ref, slots):
    rows, depth = wide_ref.shape
    part_width = acc_ref.shape[1]
    part, _ = row_ids(rows, depth, slots)
    for q in range(PARTS):
        wide = wide_ref[...]
        left = jnp.where(part == q, wide, jnp.zeros_like(wide))
        product = jnp.dot(left, weight_ref[:, pl.ds(q * part_width, part_width)], preferred_element_type=f32)
        if q == 0:
            acc_ref[...] = product
        elif q < PARTS - 1:
            acc_ref[...] += product
        else:
            product = acc_ref[...] + product
            keep_ref[...] = product[: rows // 2]
            give_ref[...] = product[rows // 2 :].astype(bf16)


def block_order(n_dp):
    return list(reversed(range(n_dp)))


def project_kernel(n_dp, slots, *refs):
    blocks = refs[:n_dp]
    up_ref, weight_ref, _, keep_ref, give_ref, rows_ref, values_ref, wide_ref, acc_ref = refs[n_dp:]
    per_rank = up_ref.shape[0]
    rows = n_dp * slots

    me_head = lax.axis_index("head")
    size = slots * per_rank
    for n, k in enumerate(block_order(n_dp)):
        place = ((k & 1) ^ me_head) * (n_dp // 2) + (k >> 1)
        x = blocks[n][...].astype(f32).reshape(size, -1)
        for c in range(rows_ref.shape[0]):
            rows_ref[c, pl.ds(pl.multiple_of(place * size, 4), size), :] = x[:, c * 128 : (c + 1) * 128]
    for j in range(per_rank):
        x = [rows_ref[c, pl.ds(j, rows, stride=per_rank), :] for c in range(rows_ref.shape[0])]
        x = jnp.concatenate(x, axis=1).astype(bf16)
        v = jnp.dot(x, up_ref[j], preferred_element_type=f32).astype(bf16)
        values_ref[:, pl.ds(j * v.shape[1], v.shape[1])] = v
    wide_ref[...] = expand(values_ref[...], slots)
    write_units(wide_ref, weight_ref, acc_ref, keep_ref, give_ref, slots)


def unit_mib(rows, part):
    return -(-8 * rows * PARTS * part * 4 // MIB)


def project(n_dp, blocks, value_up, weight, after):
    slots, per_rank, _ = blocks[0].shape
    depth, width = weight.shape
    rows = n_dp * slots
    part = width // PARTS
    own = rows * PARTS // 2
    out = lambda dtype: jax.ShapeDtypeStruct((own, part), dtype)
    return pl.pallas_call(
        functools.partial(project_kernel, n_dp, slots),
        out_shape=[out(f32), out(bf16)],
        in_specs=vmem(n_dp + 2) + [pl.BlockSpec(memory_space=pl.ANY)],
        out_specs=vmem(2),
        scratch_shapes=[
            VMEM((LATENT_WIDTH // 128, rows * per_rank, 128), f32),
            VMEM((rows, depth), bf16),
            VMEM((rows * PARTS, depth), bf16),
            VMEM((rows * PARTS, part), f32),
        ],
        compiler_params=params(unit_mib(rows, part)),
        name="project",
    )(*blocks, value_up, weight, after)


def add_kernel(n_units, keep_ref, got_ref, *outs):
    unit = outs[0].shape[0]
    for s in range(n_units):
        at = pl.ds(s * unit, unit)
        total = keep_ref[at, :] + got_ref[at, :].astype(f32)
        outs[s][...] = total.astype(bf16)
        if s == 0:
            outs[n_units][...] = total


def add_halves(n_units, keep, got):
    unit = keep.shape[0] // n_units
    shape = lambda dtype: jax.ShapeDtypeStruct((unit, keep.shape[1]), dtype)
    return pl.pallas_call(
        functools.partial(add_kernel, n_units),
        out_shape=[shape(bf16)] * n_units + [shape(f32)],
        in_specs=vmem(2),
        out_specs=vmem(n_units + 1),
        compiler_params=params(4),
        name="add_halves",
    )(keep, got)


def sum_kernel(n_units, *refs):
    own_ref, got, out_ref = refs[0], refs[1 : 1 + n_units], refs[-1]
    me_head = lax.axis_index("head")
    first = jnp.where(me_head == 0, own_ref[...], got[0][...].astype(f32))
    for ref in got[1:]:
        first = first + ref[...].astype(f32)
    out_ref[...] = first


def sum_units(own, got, after):
    return pl.pallas_call(
        functools.partial(sum_kernel, len(got)),
        out_shape=jax.ShapeDtypeStruct(own.shape, f32),
        in_specs=vmem(1 + len(got)) + [pl.BlockSpec(memory_space=pl.ANY)] * len(after),
        out_specs=vmem(1)[0],
        compiler_params=params(4),
        name="sum_units",
    )(own, *got, *after)


def prepare_kernel(slots, mine_ref, twin_ref, gain_ref, residual_ref, gains_ref):
    me_head = lax.axis_index("head")
    owner_rows = mine_ref.shape[0]
    part = residual_ref.shape[1]
    gain = gain_ref[...].reshape(1, PARTS * part)
    for q in range(PARTS):
        at = pl.ds(q * part, part)
        for ref, head in ((mine_ref, me_head), (twin_ref, 1 - me_head)):
            rows = ref[:, at].astype(f32)
            for r in range(owner_rows):
                residual_ref[pl.ds(q * slots + head * owner_rows + r, 1), :] = rows[r : r + 1]
        gains_ref[pl.ds(q * slots, slots), :] = jnp.broadcast_to(gain[:, q * part : (q + 1) * part], (slots, part))


def prepare(slots, mine, twin, gain):
    shape = jax.ShapeDtypeStruct((slots * PARTS, gain.shape[0] // PARTS), f32)
    return pl.pallas_call(
        functools.partial(prepare_kernel, slots),
        out_shape=[shape] * 2,
        in_specs=vmem(3),
        out_specs=vmem(2),
        compiler_params=params(4),
        name="prepare",
    )(mine, twin, gain)


def norm_kernel(slots, width, mine_ref, twin_ref, residual_ref, gain_ref, state_ref, normed_ref):
    state = mine_ref[...] + twin_ref[...] + residual_ref[...]
    state_ref[...] = state
    square = jnp.sum(state * state, axis=1, keepdims=True)
    rows = state.shape[0]
    _, slot = row_ids(rows, 1, slots)
    mean = jnp.zeros_like(square)
    for r in range(slots):
        total = jnp.sum(jnp.where(slot == r, square, 0.0), axis=0, keepdims=True)
        mean = jnp.where(slot == r, total, mean)
    scaled = state * lax.rsqrt(mean * (1.0 / width) + norm_epsilon)
    normed_ref[...] = (scaled * gain_ref[...]).astype(bf16)


def norm_rows(slots, mine, twin, residual, gain):
    shape = mine.shape
    return pl.pallas_call(
        functools.partial(norm_kernel, slots, shape[1] * PARTS),
        out_shape=[jax.ShapeDtypeStruct(shape, f32), jax.ShapeDtypeStruct(shape, bf16)],
        in_specs=vmem(4),
        out_specs=vmem(2),
        compiler_params=params(4),
        name="norm_rows",
    )(mine, twin, residual, gain)


def ffn_kernel(n_dp, slots, *refs):
    half = n_dp // 2
    normed_ref = refs[0]
    own, other = refs[1 : 1 + half], refs[1 + half : 1 + n_dp]
    gate_ref, up_ref, down_ref, keep_ref, give_ref, units_ref, wide_ref, acc_ref = refs[1 + n_dp :]
    rows = n_dp * slots
    unit, part = normed_ref.shape
    me_head = lax.axis_index("head")
    for s in range(half):
        mine, twins = own[s][...], other[s][...]
        if s == 0:
            mine = jnp.where(me_head == 0, normed_ref[...], mine)
            twins = jnp.where(me_head == 0, twins, normed_ref[...])
        units_ref[pl.ds(s * unit, unit), :] = mine
        units_ref[pl.ds((half + s) * unit, unit), :] = twins
    i = lax.broadcasted_iota(jnp.int32, (rows, rows * PARTS), 0).astype(f32)
    j = lax.broadcasted_iota(jnp.int32, (rows, rows * PARTS), 1).astype(f32)
    block = jnp.floor((i + 0.5) / slots)
    first = block * float(unit) + (i - block * slots)
    contract = (((1,), (1,)), ((), ()))
    gate = up = None
    for q in range(PARTS):
        pick = (first + float(q * slots) == j).astype(bf16)
        x = jnp.dot(pick, units_ref[...], preferred_element_type=f32).astype(bf16)
        at = pl.ds(q * part, part)
        gate_q = lax.dot_general(x, gate_ref[:, at], contract, preferred_element_type=f32)
        up_q = lax.dot_general(x, up_ref[:, at], contract, preferred_element_type=f32)
        gate = gate_q if q == 0 else gate + gate_q
        up = up_q if q == 0 else up + up_q
    hidden = (gate / (1.0 + jnp.exp(-gate)) * up).astype(bf16)
    wide_ref[...] = expand(hidden, slots)
    write_units(wide_ref, down_ref, acc_ref, keep_ref, give_ref, slots)


def feed_forward(n_dp, slots, normed, own, other, gate_t, up_t, down):
    _, part = normed.shape
    rows = n_dp * slots
    hidden = gate_t.shape[0]
    out = lambda dtype: jax.ShapeDtypeStruct((rows * PARTS // 2, part), dtype)
    return pl.pallas_call(
        functools.partial(ffn_kernel, n_dp, slots),
        out_shape=[out(f32), out(bf16)],
        in_specs=vmem(1 + n_dp + 3),
        out_specs=vmem(2),
        scratch_shapes=[
            VMEM((rows * PARTS, part), bf16),
            VMEM((rows * PARTS, hidden), bf16),
            VMEM((rows * PARTS, part), f32),
        ],
        compiler_params=params(unit_mib(rows, part)),
        name="feed_forward",
    )(normed, *own, *other, gate_t, up_t, down)


def final_kernel(slots, owner_rows, counts_ref, mine_ref, twin_ref, state_ref, out_ref):
    me, me_head = lax.axis_index("dp"), lax.axis_index("head")
    total = state_ref[...] + (mine_ref[...] + twin_ref[...])
    rows = total.shape[0]
    _, slot = row_ids(rows, 1, slots)
    total = jnp.where(slot < counts_ref[me].astype(f32), total, 0.0).astype(bf16)
    part = total.shape[1]
    padded = 8
    i = lax.broadcasted_iota(jnp.int32, (padded, rows), 0)
    j = lax.broadcasted_iota(jnp.int32, (padded, rows), 1)
    for q in range(PARTS):
        pick = (j == q * slots + me_head * owner_rows + i).astype(bf16)
        chosen = jnp.dot(pick, total, preferred_element_type=f32)
        out_ref[:, pl.ds(q * part, part)] = chosen[:owner_rows].astype(bf16)


def final_rows(slots, owner_rows, counts, mine, twin, state):
    return pl.pallas_call(
        functools.partial(final_kernel, slots, owner_rows),
        out_shape=jax.ShapeDtypeStruct((owner_rows, mine.shape[1] * PARTS), bf16),
        in_specs=[pl.BlockSpec(memory_space=pltpu.SMEM)] + vmem(3),
        out_specs=vmem(1)[0],
        compiler_params=params(4),
        name="final_rows",
    )(counts, mine, twin, state)


def on_device(n_dp, queries, latent_key_cache, lengths, counts, residual, value_up_weight,
              output_proj, norm_gain, gate_weight, up_weight, down_weight):
    slots = queries.shape[0]
    owner_rows = residual.shape[0]
    half = n_dp // 2

    def to_peer(x, k):
        return lax.ppermute(x, "dp", [(i, i ^ k) for i in range(n_dp)])

    def to_twin(x):
        return lax.ppermute(x, "head", [(0, 1), (1, 0)])

    def to_set(x, s):
        pairs = [(2 * i + h, 2 * (i ^ (2 * s + h)) + h) for i in range(n_dp) for h in range(2) if 2 * s + h]
        return lax.ppermute(x, ("dp", "head"), pairs)

    def reduce_units(keep, give, weights):
        units = add_halves(half, keep, to_twin(give))
        weights = load(units[half], weights, 2) if weights else []
        mine = sum_units(units[half], [to_set(units[s], s) for s in range(half)], weights)
        return mine, to_twin(mine), weights

    residual_unit, gain_unit = prepare(slots, residual, to_twin(residual), norm_gain)
    outs = attend(n_dp, counts, lengths, queries, latent_key_cache, [value_up_weight[0], output_proj[0]])
    blocks, (value_up, proj) = outs[:n_dp], outs[n_dp:]
    (gate,) = load(blocks[0], [gate_weight.T], 2)
    blocks = [to_peer(blocks[k], k) if k else blocks[0] for k in block_order(n_dp)]
    keep, give = project(n_dp, blocks, value_up, proj, gate)
    mine, twin, (up, down) = reduce_units(keep, give, [up_weight.T, down_weight])
    state, normed = norm_rows(slots, mine, twin, residual_unit, gain_unit)
    own = [to_set(normed, s) for s in range(half)]
    other = [to_twin(x) for x in own]
    keep, give = feed_forward(n_dp, slots, normed, own, other, gate, up, down)
    mine, twin, _ = reduce_units(keep, give, [])
    return final_rows(slots, owner_rows, counts, mine, twin, state)


def solution(mesh):
    n_dp = mesh.shape["dp"]
    in_specs = (
        P(("groups", "dp"), "head", None),
        P(("groups", "dp"), None, None),
        P(("groups", "dp")),
        P("groups"),
        P(("groups", "dp", "head"), None),
        P("head", "dp", None, None),
        P("head", "dp", None),
        P(),
        P(None, ("dp", "head")),
        P(None, ("dp", "head")),
        P(("dp", "head"), None),
    )
    out_specs = P(("groups", "dp", "head"), None)

    def step(*args):
        return on_device(n_dp, *args)

    return jax.shard_map(step, mesh=mesh, in_specs=in_specs, out_specs=out_specs, check_vma=False)
```

```python
import functools

import jax
import jax.numpy as jnp
from jax import lax
from jax.experimental import pallas as pl
from jax.experimental.pallas import tpu as pltpu
from jax.sharding import PartitionSpec as P

LATENT_WIDTH = 512
PIECES = 8
PARTS = 4

score_scale = 0.07216878364870322
norm_epsilon = 1e-06
masked_score = -1e30
f32 = jnp.float32
bf16 = jnp.bfloat16
VMEM = pltpu.VMEM
MIB = 1 << 20


def in_hbm(arrays):
    return [pltpu.with_memory_space_constraint(x, pltpu.HBM) for x in arrays]


def vmem(n):
    return [pl.BlockSpec(memory_space=VMEM)] * n


def params(mib):
    return pltpu.CompilerParams(vmem_limit_bytes=mib * MIB)


def piece_count(rows, most):
    return next(p for p in range(most, 0, -1) if p == 1 or rows % (8 * p) == 0)


def piece_copies(source, target, sems):
    count = sems.shape[0]
    if len(source.shape) == 2:
        count = piece_count(source.shape[0], count)
    step = source.shape[0] // count
    copies = []
    for p in range(count):
        at = pl.ds(p * step, step)
        here = source.at[at]
        if target.shape != source.shape:
            here = source.at[at, pl.ds(0, target.shape[1])]
        copies.append(pltpu.make_async_copy(here, target.at[at], sems.at[p]))
    return copies


def load_kernel(_, source, target, sems):
    copies = piece_copies(source, target, sems)
    for copy in copies:
        copy.start()
    for copy in copies:
        copy.wait()


def load(after, weight):
    return pl.pallas_call(
        load_kernel,
        out_shape=jax.ShapeDtypeStruct(weight.shape, weight.dtype),
        in_specs=[pl.BlockSpec(memory_space=pl.ANY)] * 2,
        out_specs=vmem(1)[0],
        scratch_shapes=[pltpu.SemaphoreType.DMA((PIECES,))],
        compiler_params=params(2),
        cost_estimate=pl.CostEstimate(flops=0, bytes_accessed=4 * weight.size, transcendentals=0),
        name="load",
    )(after, *in_hbm([weight]))


def row_ids(rows, columns, slots):
    i = lax.broadcasted_iota(jnp.int32, (rows, columns), 0).astype(f32)
    unit = float(slots * PARTS)
    block = jnp.floor((i + 0.5) / unit)
    inner = i - block * unit
    part = jnp.floor((inner + 0.5) / slots)
    return part, block * slots + (inner - part * slots)


def attention_kernel(n_dp, counts_hbm, lengths_hbm, q_hbm, cache_hbm, residual_hbm, gain_hbm, *refs):
    n_weights = 2
    weights, outs = refs[:n_weights], refs[n_weights : n_weights + n_dp]
    residual_unit, gain_unit, to_heads, to_units, to_parts = refs[n_weights + n_dp : n_weights + n_dp + 5]
    loaded = refs[n_weights + n_dp + 5 : 2 * n_weights + n_dp + 5]
    counts_ref, lengths_ref, q_ref, cache_ref, residual_ref, gain_ref, held, sems, weight_sems = refs[
        2 * n_weights + n_dp + 5 :
    ]
    slots = q_ref.shape[0]
    pairs = [
        (counts_hbm, counts_ref),
        (lengths_hbm, lengths_ref),
        (q_hbm, q_ref),
        (cache_hbm, cache_ref),
        (residual_hbm, residual_ref),
        (gain_hbm, gain_ref),
    ]
    copies = [pltpu.make_async_copy(src, dst, sems.at[n]) for n, (src, dst) in enumerate(pairs)]
    fetches = []
    for n in range(n_weights):
        fetches += piece_copies(weights[n], loaded[n], weight_sems.at[n])
    for copy in copies + fetches:
        copy.start()
    me, me_head = lax.axis_index("dp"), lax.axis_index("head")
    for copy in copies:
        copy.wait()
    rows = range(slots)
    scores = []
    for row in rows:
        score = lax.dot_general(q_ref[row], cache_ref[row], (((1,), (1,)), ((), ())), preferred_element_type=f32)
        position = lax.broadcasted_iota(jnp.int32, score.shape, 1)
        scores.append(jnp.where(position < lengths_ref[row], score * score_scale, masked_score))
    probs = [jnp.exp(x - jnp.max(x, axis=-1, keepdims=True)) for x in scores]
    for row in rows:
        weighted = jnp.dot(probs[row].astype(bf16), cache_ref[row, :, :LATENT_WIDTH], preferred_element_type=f32)
        denominator = jnp.sum(probs[row], axis=-1, keepdims=True)
        latent = jnp.where(row < counts_ref[me], weighted / denominator, 0.0).astype(bf16)
        held[row] = latent.reshape(held.shape[1:])
    for k in range(n_dp):
        for row in rows:
            outs[k][row] = held[row, me ^ k]
    to_heads[...] = regroup(to_heads.shape[0], held.shape[2], n_dp * slots)
    to_units[...] = regroup(to_units.shape[0], n_dp // 2, PARTS)
    to_parts[...] = regroup(to_parts.shape[0], PARTS, n_dp)
    owner_rows = residual_ref.shape[0]
    part = residual_unit.shape[1]
    gain = gain_ref[...].reshape(1, PARTS * part)
    residual_unit[...] = jnp.zeros_like(residual_unit)
    for q in range(PARTS):
        at = pl.ds(q * part, part)
        mine = residual_ref[:, at].astype(f32)
        for r in range(owner_rows):
            residual_unit[pl.ds(q * slots + me_head * owner_rows + r, 1), :] = mine[r : r + 1]
        gain_unit[pl.ds(q * slots, slots), :] = jnp.broadcast_to(gain[:, q * part : (q + 1) * part], (slots, part))
    for copy in fetches:
        copy.wait()


def attend(n_dp, counts, lengths, queries, cache, residual, gain, value_up, proj):
    slots, heads, _ = queries.shape
    per_rank = heads // n_dp
    part = gain.shape[0] // PARTS
    block = jax.ShapeDtypeStruct((slots, per_rank, LATENT_WIDTH), bf16)
    unit = jax.ShapeDtypeStruct((slots * PARTS, part), f32)
    rows = n_dp * slots
    moves = [jax.ShapeDtypeStruct((n, n), bf16) for n in (rows * per_rank, rows * PARTS // 2, rows * PARTS)]
    loaded = [
        jax.ShapeDtypeStruct(value_up.shape, bf16),
        jax.ShapeDtypeStruct((proj.shape[0], part * (PARTS - 1)), bf16),
    ]
    return pl.pallas_call(
        functools.partial(attention_kernel, n_dp),
        out_shape=[block] * n_dp + [unit] * 2 + moves + loaded,
        in_specs=[pl.BlockSpec(memory_space=pl.ANY)] * 8,
        out_specs=vmem(n_dp + 7),
        scratch_shapes=[
            pltpu.SMEM(counts.shape, jnp.int32),
            pltpu.SMEM(lengths.shape, jnp.int32),
            VMEM(queries.shape, bf16),
            VMEM(cache.shape, bf16),
            VMEM(residual.shape, bf16),
            VMEM(gain.shape, f32),
            VMEM((slots, n_dp, per_rank, LATENT_WIDTH), bf16),
            pltpu.SemaphoreType.DMA((6,)),
            pltpu.SemaphoreType.DMA((2, 2)),
        ],
        compiler_params=params(10),
        name="attend",
    )(*in_hbm([counts, lengths, queries, cache, residual, gain, value_up, proj]))


def write_parts(x, weight_part, keep_ref, give_ref):
    half = x.shape[0] // 2
    for q in range(PARTS):
        product = jnp.dot(x, weight_part(q), preferred_element_type=f32)
        at = pl.ds(q * half, half)
        keep_ref[at, :] = product[:half]
        give_ref[at, :] = product[half:].astype(bf16)


def regroup(rows, inner, outer):
    slots = rows // (inner * outer)
    i = lax.broadcasted_iota(jnp.int32, (rows, rows), 0).astype(f32)
    j = lax.broadcasted_iota(jnp.int32, (rows, rows), 1).astype(f32)
    b = jnp.floor((i + 0.5) / (outer * slots))
    rest = i - b * (outer * slots)
    a = jnp.floor((rest + 0.5) / slots)
    return (a * (inner * slots) + b * slots + (rest - a * slots) == j).astype(bf16)


def move_rows(matrix, x):
    return jnp.dot(matrix, x, preferred_element_type=f32).astype(bf16)


def block_order(n_dp):
    far = list(range(n_dp // 2, n_dp))
    return [*far[::-1][1::2], *far[::-1][::2], *reversed(range(n_dp // 2))]


def set_order(half):
    return [*range(half // 2, half), *reversed(range(half // 2))]


def project_kernel(n_dp, slots, *refs):
    blocks = refs[:n_dp]
    up_ref, weight_ref, move_ref, weight_hbm, _, keep_ref, give_ref, last_ref, rows_ref, values_ref, sems = refs[n_dp:]
    per_rank = up_ref.shape[0]
    rows = n_dp * slots
    width = last_ref.shape[1]
    copies = piece_copies(weight_hbm.at[:, pl.ds((PARTS - 1) * width, width)], last_ref, sems)
    for copy in copies:
        copy.start()
    me_head = lax.axis_index("head")
    size = slots * per_rank
    for n, k in enumerate(block_order(n_dp)):
        place = ((k & 1) ^ me_head) * (n_dp // 2) + (k >> 1)
        x = blocks[n][...].reshape(size, -1)
        if size % 8 == 0:
            rows_ref[pl.ds(pl.multiple_of(place * size, 8), size), :] = x
        else:
            x = x.astype(f32)
            for c in range(rows_ref.shape[0]):
                rows_ref[c, pl.ds(pl.multiple_of(place * size, 4), size), :] = x[:, c * 128 : (c + 1) * 128]
    if size % 8 == 0:
        gathered = rows_ref[...]
    else:
        gathered = jnp.concatenate([rows_ref[c] for c in range(rows_ref.shape[0])], axis=1).astype(bf16)
    by_head = move_rows(move_ref[...], gathered)
    for j in range(per_rank):
        v = jnp.dot(by_head[j * rows : (j + 1) * rows], up_ref[j], preferred_element_type=f32).astype(bf16)
        values_ref[:, pl.ds(j * v.shape[1], v.shape[1])] = v

    def weight_part(q):
        if q < PARTS - 1:
            return weight_ref[:, pl.ds(q * width, width)]
        for copy in copies:
            copy.wait()
        return last_ref[...]

    write_parts(values_ref[...], weight_part, keep_ref, give_ref)


def unit_mib(rows, part):
    return -(-8 * rows * PARTS * part * 4 // MIB)


def project(n_dp, blocks, value_up, most, move, weight, after):
    slots, per_rank, _ = blocks[0].shape
    depth, width = weight.shape
    rows = n_dp * slots
    part = width // PARTS
    own = rows * PARTS // 2
    out = lambda dtype: jax.ShapeDtypeStruct((own, part), dtype)
    gathered = VMEM((rows * per_rank, LATENT_WIDTH), bf16)
    if slots * per_rank % 8:
        gathered = VMEM((LATENT_WIDTH // 128, rows * per_rank, 128), f32)
    return pl.pallas_call(
        functools.partial(project_kernel, n_dp, slots),
        out_shape=[out(f32), out(bf16)],
        in_specs=vmem(n_dp + 3) + [pl.BlockSpec(memory_space=pl.ANY)] * 2,
        out_specs=vmem(2),
        scratch_shapes=[
            VMEM((depth, part), bf16),
            gathered,
            VMEM((rows, depth), bf16),
            pltpu.SemaphoreType.DMA((PIECES,)),
        ],
        compiler_params=params(unit_mib(rows, part) + 4),
        name="project",
    )(*blocks, value_up, most, move, *in_hbm([weight]), after)


def add_kernel(n_units, keep_ref, got_ref, move_ref, *outs):
    total = (keep_ref[...] + got_ref[...].astype(f32)).astype(bf16)
    units = move_rows(move_ref[...], total)
    size = units.shape[0] // n_units
    for s in range(n_units):
        outs[s][...] = units[s * size : (s + 1) * size]


def add_halves(n_units, keep, got, move):
    unit = keep.shape[0] // n_units
    return pl.pallas_call(
        functools.partial(add_kernel, n_units),
        out_shape=[jax.ShapeDtypeStruct((unit, keep.shape[1]), bf16)] * n_units,
        in_specs=vmem(3),
        out_specs=vmem(n_units),
        compiler_params=params(unit_mib(keep.shape[0] // PARTS, keep.shape[1])),
        name="add_halves",
    )(keep, got, move)


def sum_kernel(n_units, own_ref, base_ref, *refs):
    got, out_ref = refs[:n_units], refs[-1]
    me_head = lax.axis_index("head")
    zeroth = set_order(n_units).index(0)
    total = base_ref[...] + jnp.where(me_head == 0, own_ref[...], got[zeroth][...]).astype(f32)
    for ref in got[:zeroth] + got[zeroth + 1 :]:
        total = total + ref[...].astype(f32)
    out_ref[...] = total


def sum_units(own, base, got, after):
    return pl.pallas_call(
        functools.partial(sum_kernel, len(got)),
        out_shape=jax.ShapeDtypeStruct(own.shape, f32),
        in_specs=vmem(2 + len(got)) + [pl.BlockSpec(memory_space=pl.ANY)] * len(after),
        out_specs=vmem(1)[0],
        compiler_params=params(4),
        name="sum_units",
    )(own, base, *got, *after)


def norm_kernel(slots, width, mine_ref, twin_ref, gain_ref, state_ref, normed_ref):
    state = mine_ref[...] + twin_ref[...]
    square = jnp.sum(state * state, axis=1, keepdims=True)
    rows = state.shape[0]
    _, slot = row_ids(rows, 1, slots)
    first = (lax.axis_index("head") * (slots // 2)).astype(f32)
    owned = (slot >= first) & (slot < first + slots // 2)
    state_ref[...] = jnp.where(owned, state, 0.0)
    mean = jnp.zeros_like(square)
    for r in range(slots):
        total = jnp.sum(jnp.where(slot == r, square, 0.0), axis=0, keepdims=True)
        mean = jnp.where(slot == r, total, mean)
    scaled = state * lax.rsqrt(mean * (1.0 / width) + norm_epsilon)
    normed_ref[...] = (scaled * gain_ref[...]).astype(bf16)


def norm_rows(slots, mine, twin, gain):
    shape = mine.shape
    return pl.pallas_call(
        functools.partial(norm_kernel, slots, shape[1] * PARTS),
        out_shape=[jax.ShapeDtypeStruct(shape, f32), jax.ShapeDtypeStruct(shape, bf16)],
        in_specs=vmem(3),
        out_specs=vmem(2),
        compiler_params=params(4),
        name="norm_rows",
    )(mine, twin, gain)


def ffn_kernel(n_dp, slots, *refs):
    half = n_dp // 2
    normed_ref = refs[0]
    own, other = refs[1 : 1 + half], refs[1 + half : 1 + n_dp]
    gate_ref, up_ref, down_ref, move_ref, keep_ref, give_ref, units_ref, rows_ref = refs[1 + n_dp :]
    rows = n_dp * slots
    unit, part = normed_ref.shape
    me_head = lax.axis_index("head")
    for s in range(half):
        mine, twins = own[s][...], other[s][...]
        if s == 0:
            mine = jnp.where(me_head == 0, normed_ref[...], mine)
            twins = jnp.where(me_head == 0, twins, normed_ref[...])
        units_ref[pl.ds(s * unit, unit), :] = mine
        units_ref[pl.ds((half + s) * unit, unit), :] = twins
    moved = move_rows(move_ref[...], units_ref[...])
    for q in range(PARTS):
        rows_ref[:, pl.ds(q * part, part)] = moved[q * rows : (q + 1) * rows]
    x = rows_ref[...]
    contract = (((1,), (1,)), ((), ()))
    gate = lax.dot_general(x, gate_ref[...], contract, preferred_element_type=f32)
    up = lax.dot_general(x, up_ref[...], contract, preferred_element_type=f32)
    hidden = (gate / (1.0 + jnp.exp(-gate)) * up).astype(bf16)
    write_parts(hidden, lambda q: down_ref[:, pl.ds(q * part, part)], keep_ref, give_ref)


def feed_forward(n_dp, slots, normed, own, other, gate_t, up_t, down, move):
    _, part = normed.shape
    rows = n_dp * slots
    out = lambda dtype: jax.ShapeDtypeStruct((rows * PARTS // 2, part), dtype)
    return pl.pallas_call(
        functools.partial(ffn_kernel, n_dp, slots),
        out_shape=[out(f32), out(bf16)],
        in_specs=vmem(1 + n_dp + 4),
        out_specs=vmem(2),
        scratch_shapes=[VMEM((rows * PARTS, part), bf16), VMEM((rows, PARTS * part), bf16)],
        compiler_params=params(unit_mib(rows, part)),
        name="feed_forward",
    )(normed, *own, *other, gate_t, up_t, down, move)


def final_kernel(slots, owner_rows, counts_ref, mine_ref, twin_ref, out_ref):
    me, me_head = lax.axis_index("dp"), lax.axis_index("head")
    total = mine_ref[...] + twin_ref[...]
    rows = total.shape[0]
    _, slot = row_ids(rows, 1, slots)
    total = jnp.where(slot < counts_ref[me].astype(f32), total, 0.0).astype(bf16)
    part = total.shape[1]
    padded = 8
    i = lax.broadcasted_iota(jnp.int32, (padded, rows), 0)
    j = lax.broadcasted_iota(jnp.int32, (padded, rows), 1)
    for q in range(PARTS):
        pick = (j == q * slots + me_head * owner_rows + i).astype(bf16)
        chosen = jnp.dot(pick, total, preferred_element_type=f32)
        out_ref[:, pl.ds(q * part, part)] = chosen[:owner_rows].astype(bf16)


def final_rows(slots, owner_rows, counts, mine, twin):
    return pl.pallas_call(
        functools.partial(final_kernel, slots, owner_rows),
        out_shape=jax.ShapeDtypeStruct((owner_rows, mine.shape[1] * PARTS), bf16),
        in_specs=[pl.BlockSpec(memory_space=pltpu.SMEM)] + vmem(2),
        out_specs=vmem(1)[0],
        compiler_params=params(4),
        name="final_rows",
    )(counts, mine, twin)


def on_device(n_dp, queries, latent_key_cache, lengths, counts, residual, value_up_weight,
              output_proj, norm_gain, gate_weight, up_weight, down_weight):
    slots = queries.shape[0]
    owner_rows = residual.shape[0]
    half = n_dp // 2

    def to_peer(x, k):
        return lax.ppermute(x, "dp", [(i, i ^ k) for i in range(n_dp)])

    def to_twin(x):
        return lax.ppermute(x, "head", [(0, 1), (1, 0)])

    def to_set(x, s):
        pairs = [(2 * i + h, 2 * (i ^ (2 * s + h)) + h) for i in range(n_dp) for h in range(2) if 2 * s + h]
        return lax.ppermute(x, ("dp", "head"), pairs)

    outs = attend(
        n_dp, counts, lengths, queries, latent_key_cache, residual, norm_gain, value_up_weight[0], output_proj[0]
    )
    blocks, (residual_unit, gain_unit, to_heads, to_units, to_parts, value_up, most) = outs[:n_dp], outs[n_dp:]
    def reduce_units(keep, give, base, weights):
        units = add_halves(half, keep, to_twin(give), to_units)
        weights = [load(units[0], w) for w in weights]
        got = [to_set(units[s], s) for s in set_order(half)]
        mine = sum_units(units[0], base, got, weights)
        return mine, to_twin(mine), weights

    gate = load(blocks[0], gate_weight.T)
    blocks = [to_peer(blocks[k], k) if k else blocks[0] for k in block_order(n_dp)]
    keep, give = project(n_dp, blocks, value_up, most, to_heads, output_proj[0], gate)
    mine, twin, (up,) = reduce_units(keep, give, residual_unit, [up_weight.T])
    state, normed = norm_rows(slots, mine, twin, gain_unit)
    down = load(normed, down_weight)
    own = {s: to_set(normed, s) for s in reversed(set_order(half))}
    tied = set_order(half)[1]
    own[tied], down = lax.optimization_barrier((own[tied], down))
    other = {s: to_twin(own[s]) for s in set_order(half)}
    own, other = [own[s] for s in range(half)], [other[s] for s in range(half)]
    keep, give = feed_forward(n_dp, slots, normed, own, other, gate, up, down, to_parts)
    mine, twin, _ = reduce_units(keep, give, state, [])
    return final_rows(slots, owner_rows, counts, mine, twin)


def solution(mesh):
    n_dp = mesh.shape["dp"]
    in_specs = (
        P(("groups", "dp"), "head", None),
        P(("groups", "dp"), None, None),
        P(("groups", "dp")),
        P("groups"),
        P(("groups", "dp", "head"), None),
        P("head", "dp", None, None),
        P("head", "dp", None),
        P(),
        P(None, ("dp", "head")),
        P(None, ("dp", "head")),
        P(("dp", "head"), None),
    )
    out_specs = P(("groups", "dp", "head"), None)

    def step(*args):
        return on_device(n_dp, *args)

    return jax.shard_map(step, mesh=mesh, in_specs=in_specs, out_specs=out_specs, check_vma=False)
```

```python
import functools

import jax
import jax.numpy as jnp
from jax import lax
from jax.experimental import pallas as pl
from jax.experimental.pallas import tpu as pltpu
from jax.sharding import PartitionSpec as P

LATENT_WIDTH = 512
PIECES = 8
PARTS = 4

score_scale = 0.07216878364870322
norm_epsilon = 1e-06
masked_score = -1e30
f32 = jnp.float32
bf16 = jnp.bfloat16
VMEM = pltpu.VMEM
MIB = 1 << 20


def in_hbm(arrays):
    return [pltpu.with_memory_space_constraint(x, pltpu.HBM) for x in arrays]


def vmem(n):
    return [pl.BlockSpec(memory_space=VMEM)] * n


def params(mib):
    return pltpu.CompilerParams(vmem_limit_bytes=mib * MIB)


def piece_count(rows, most):
    return next(p for p in range(most, 0, -1) if p == 1 or rows % (8 * p) == 0)


def piece_copies(source, target, sems):
    count = sems.shape[0]
    if len(source.shape) == 2:
        count = piece_count(source.shape[0], count)
    step = source.shape[0] // count
    copies = []
    for p in range(count):
        at = pl.ds(p * step, step)
        here = source.at[at]
        if target.shape != source.shape:
            here = source.at[at, pl.ds(0, target.shape[1])]
        copies.append(pltpu.make_async_copy(here, target.at[at], sems.at[p]))
    return copies


def load_kernel(_, source, target, sems):
    copies = piece_copies(source, target, sems)
    for copy in copies:
        copy.start()
    for copy in copies:
        copy.wait()


def load(after, weight):
    return pl.pallas_call(
        load_kernel,
        out_shape=jax.ShapeDtypeStruct(weight.shape, weight.dtype),
        in_specs=[pl.BlockSpec(memory_space=pl.ANY)] * 2,
        out_specs=vmem(1)[0],
        scratch_shapes=[pltpu.SemaphoreType.DMA((PIECES,))],
        compiler_params=params(2),
        cost_estimate=pl.CostEstimate(flops=0, bytes_accessed=4 * weight.size, transcendentals=0),
        name="load",
    )(after, *in_hbm([weight]))


def row_ids(rows, columns, slots):
    i = lax.broadcasted_iota(jnp.int32, (rows, columns), 0).astype(f32)
    unit = float(slots * PARTS)
    block = jnp.floor((i + 0.5) / unit)
    inner = i - block * unit
    part = jnp.floor((inner + 0.5) / slots)
    return part, block * slots + (inner - part * slots)


def attention_kernel(n_dp, counts_hbm, lengths_hbm, q_hbm, cache_hbm, residual_hbm, gain_hbm, *refs):
    n_weights = 2
    weights, outs = refs[:n_weights], refs[n_weights : n_weights + n_dp]
    residual_unit, gain_unit, live_ref, to_heads, to_units, to_parts = refs[n_weights + n_dp : n_weights + n_dp + 6]
    loaded = refs[n_weights + n_dp + 6 : 2 * n_weights + n_dp + 6]
    counts_ref, lengths_ref, q_ref, cache_ref, residual_ref, gain_ref, held, sems, weight_sems = refs[
        2 * n_weights + n_dp + 6 :
    ]
    slots = q_ref.shape[0]
    pairs = [
        (counts_hbm, counts_ref),
        (lengths_hbm, lengths_ref),
        (q_hbm, q_ref),
        (cache_hbm, cache_ref),
        (residual_hbm, residual_ref),
        (gain_hbm, gain_ref),
    ]
    copies = [pltpu.make_async_copy(src, dst, sems.at[n]) for n, (src, dst) in enumerate(pairs)]
    fetches = []
    for n in range(n_weights):
        fetches += piece_copies(weights[n], loaded[n], weight_sems.at[n])
    for copy in copies + fetches:
        copy.start()
    me, me_head = lax.axis_index("dp"), lax.axis_index("head")
    for copy in copies:
        copy.wait()
    rows = range(slots)
    scores = []
    for row in rows:
        score = lax.dot_general(q_ref[row], cache_ref[row], (((1,), (1,)), ((), ())), preferred_element_type=f32)
        position = lax.broadcasted_iota(jnp.int32, score.shape, 1)
        scores.append(jnp.where(position < lengths_ref[row], score * score_scale, masked_score))
    probs = [jnp.exp(x - jnp.max(x, axis=-1, keepdims=True)) for x in scores]
    for row in rows:
        weighted = jnp.dot(probs[row].astype(bf16), cache_ref[row, :, :LATENT_WIDTH], preferred_element_type=f32)
        denominator = jnp.sum(probs[row], axis=-1, keepdims=True)
        latent = jnp.where(row < counts_ref[me], weighted / denominator, 0.0).astype(bf16)
        held[row] = latent.reshape(held.shape[1:])
    for k in range(n_dp):
        for row in rows:
            outs[k][row] = held[row, me ^ k]
    _, slot = row_ids(*live_ref.shape, slots)
    live_ref[...] = (slot < counts_ref[me].astype(f32)).astype(f32)
    to_heads[...] = regroup(to_heads.shape[0], held.shape[2], n_dp * slots)
    to_units[...] = regroup(to_units.shape[0], n_dp // 2, PARTS)
    to_parts[...] = regroup(to_parts.shape[0], PARTS, n_dp)
    owner_rows = residual_ref.shape[0]
    part = residual_unit.shape[1]
    gain = gain_ref[...].reshape(1, PARTS * part)
    residual_unit[...] = jnp.zeros_like(residual_unit)
    for q in range(PARTS):
        at = pl.ds(q * part, part)
        mine = residual_ref[:, at].astype(f32)
        for r in range(owner_rows):
            residual_unit[pl.ds(q * slots + me_head * owner_rows + r, 1), :] = mine[r : r + 1]
        gain_unit[pl.ds(q * slots, slots), :] = jnp.broadcast_to(gain[:, q * part : (q + 1) * part], (slots, part))
    for copy in fetches:
        copy.wait()


def attend(n_dp, counts, lengths, queries, cache, residual, gain, value_up, proj):
    slots, heads, _ = queries.shape
    per_rank = heads // n_dp
    part = gain.shape[0] // PARTS
    block = jax.ShapeDtypeStruct((slots, per_rank, LATENT_WIDTH), bf16)
    unit = jax.ShapeDtypeStruct((slots * PARTS, part), f32)
    rows = n_dp * slots
    live = jax.ShapeDtypeStruct((slots * PARTS, 128), f32)
    moves = [jax.ShapeDtypeStruct((n, n), bf16) for n in (rows * per_rank, rows * PARTS // 2, rows * PARTS)]
    loaded = [
        jax.ShapeDtypeStruct(value_up.shape, bf16),
        jax.ShapeDtypeStruct((proj.shape[0], part * (PARTS - 1)), bf16),
    ]
    return pl.pallas_call(
        functools.partial(attention_kernel, n_dp),
        out_shape=[block] * n_dp + [unit] * 2 + [live] + moves + loaded,
        in_specs=[pl.BlockSpec(memory_space=pl.ANY)] * 8,
        out_specs=vmem(n_dp + 8),
        scratch_shapes=[
            pltpu.SMEM(counts.shape, jnp.int32),
            pltpu.SMEM(lengths.shape, jnp.int32),
            VMEM(queries.shape, bf16),
            VMEM(cache.shape, bf16),
            VMEM(residual.shape, bf16),
            VMEM(gain.shape, f32),
            VMEM((slots, n_dp, per_rank, LATENT_WIDTH), bf16),
            pltpu.SemaphoreType.DMA((6,)),
            pltpu.SemaphoreType.DMA((2, 2)),
        ],
        compiler_params=params(10),
        name="attend",
    )(*in_hbm([counts, lengths, queries, cache, residual, gain, value_up, proj]))


def write_parts(x, weight_part, keep_ref, give_ref):
    half = x.shape[0] // 2
    for q in range(PARTS):
        product = jnp.dot(x, weight_part(q), preferred_element_type=f32)
        at = pl.ds(q * half, half)
        keep_ref[at, :] = product[:half]
        give_ref[at, :] = product[half:].astype(bf16)


def regroup(rows, inner, outer):
    slots = rows // (inner * outer)
    i = lax.broadcasted_iota(jnp.int32, (rows, rows), 0).astype(f32)
    j = lax.broadcasted_iota(jnp.int32, (rows, rows), 1).astype(f32)
    b = jnp.floor((i + 0.5) / (outer * slots))
    rest = i - b * (outer * slots)
    a = jnp.floor((rest + 0.5) / slots)
    return (a * (inner * slots) + b * slots + (rest - a * slots) == j).astype(bf16)


def move_rows(matrix, x):
    return jnp.dot(matrix, x, preferred_element_type=f32).astype(bf16)


def block_order(n_dp):
    far = list(range(n_dp // 2, n_dp))
    return [*far[::-1][1::2], *far[::-1][::2], *reversed(range(n_dp // 2))]


def set_order(half):
    return [*range(half // 2, half), *reversed(range(half // 2))]


def project_kernel(n_dp, slots, *refs):
    blocks = refs[:n_dp]
    up_ref, weight_ref, move_ref, weight_hbm, _, keep_ref, give_ref, last_ref, rows_ref, values_ref, sems = refs[n_dp:]
    per_rank = up_ref.shape[0]
    rows = n_dp * slots
    width = last_ref.shape[1]
    copies = piece_copies(weight_hbm.at[:, pl.ds((PARTS - 1) * width, width)], last_ref, sems)
    for copy in copies:
        copy.start()
    me_head = lax.axis_index("head")
    size = slots * per_rank
    for n, k in enumerate(block_order(n_dp)):
        place = ((k & 1) ^ me_head) * (n_dp // 2) + (k >> 1)
        x = blocks[n][...].reshape(size, -1)
        if size % 8 == 0:
            rows_ref[pl.ds(pl.multiple_of(place * size, 8), size), :] = x
        else:
            x = x.astype(f32)
            for c in range(rows_ref.shape[0]):
                rows_ref[c, pl.ds(pl.multiple_of(place * size, 4), size), :] = x[:, c * 128 : (c + 1) * 128]
    if size % 8 == 0:
        gathered = rows_ref[...]
    else:
        gathered = jnp.concatenate([rows_ref[c] for c in range(rows_ref.shape[0])], axis=1).astype(bf16)
    by_head = move_rows(move_ref[...], gathered)
    for j in range(per_rank):
        v = jnp.dot(by_head[j * rows : (j + 1) * rows], up_ref[j], preferred_element_type=f32).astype(bf16)
        values_ref[:, pl.ds(j * v.shape[1], v.shape[1])] = v

    def weight_part(q):
        if q < PARTS - 1:
            return weight_ref[:, pl.ds(q * width, width)]
        for copy in copies:
            copy.wait()
        return last_ref[...]

    write_parts(values_ref[...], weight_part, keep_ref, give_ref)


def unit_mib(rows, part):
    return -(-8 * rows * PARTS * part * 4 // MIB)


def project(n_dp, blocks, value_up, most, move, weight, after):
    slots, per_rank, _ = blocks[0].shape
    depth, width = weight.shape
    rows = n_dp * slots
    part = width // PARTS
    own = rows * PARTS // 2
    out = lambda dtype: jax.ShapeDtypeStruct((own, part), dtype)
    gathered = VMEM((rows * per_rank, LATENT_WIDTH), bf16)
    if slots * per_rank % 8:
        gathered = VMEM((LATENT_WIDTH // 128, rows * per_rank, 128), f32)
    return pl.pallas_call(
        functools.partial(project_kernel, n_dp, slots),
        out_shape=[out(f32), out(bf16)],
        in_specs=vmem(n_dp + 3) + [pl.BlockSpec(memory_space=pl.ANY)] * 2,
        out_specs=vmem(2),
        scratch_shapes=[
            VMEM((depth, part), bf16),
            gathered,
            VMEM((rows, depth), bf16),
            pltpu.SemaphoreType.DMA((PIECES,)),
        ],
        compiler_params=params(unit_mib(rows, part) + 4),
        name="project",
    )(*blocks, value_up, most, move, *in_hbm([weight]), after)


def add_kernel(n_units, keep_ref, got_ref, move_ref, *outs):
    total = (keep_ref[...] + got_ref[...].astype(f32)).astype(bf16)
    units = move_rows(move_ref[...], total)
    size = units.shape[0] // n_units
    for s in range(n_units):
        outs[s][...] = units[s * size : (s + 1) * size]


def add_halves(n_units, keep, got, move):
    unit = keep.shape[0] // n_units
    return pl.pallas_call(
        functools.partial(add_kernel, n_units),
        out_shape=[jax.ShapeDtypeStruct((unit, keep.shape[1]), bf16)] * n_units,
        in_specs=vmem(3),
        out_specs=vmem(n_units),
        compiler_params=params(unit_mib(keep.shape[0] // PARTS, keep.shape[1])),
        name="add_halves",
    )(keep, got, move)


def sum_kernel(n_units, own_ref, base_ref, *refs):
    got, out_ref = refs[:n_units], refs[-1]
    me_head = lax.axis_index("head")
    zeroth = set_order(n_units).index(0)
    total = base_ref[...] + jnp.where(me_head == 0, own_ref[...], got[zeroth][...]).astype(f32)
    for ref in got[:zeroth] + got[zeroth + 1 :]:
        total = total + ref[...].astype(f32)
    out_ref[...] = total


def sum_units(own, base, got, after):
    return pl.pallas_call(
        functools.partial(sum_kernel, len(got)),
        out_shape=jax.ShapeDtypeStruct(own.shape, f32),
        in_specs=vmem(2 + len(got)) + [pl.BlockSpec(memory_space=pl.ANY)] * len(after),
        out_specs=vmem(1)[0],
        compiler_params=params(4),
        name="sum_units",
    )(own, base, *got, *after)


def norm_kernel(slots, width, mine_ref, twin_ref, gain_ref, state_ref, normed_ref):
    state = mine_ref[...] + twin_ref[...]
    square = jnp.sum(state * state, axis=1, keepdims=True)
    rows = state.shape[0]
    _, slot = row_ids(rows, 1, slots)
    first = (lax.axis_index("head") * (slots // 2)).astype(f32)
    owned = (slot >= first) & (slot < first + slots // 2)
    state_ref[...] = jnp.where(owned, state, 0.0)
    mean = jnp.zeros_like(square)
    for r in range(slots):
        total = jnp.sum(jnp.where(slot == r, square, 0.0), axis=0, keepdims=True)
        mean = jnp.where(slot == r, total, mean)
    scaled = state * lax.rsqrt(mean * (1.0 / width) + norm_epsilon)
    normed_ref[...] = (scaled * gain_ref[...]).astype(bf16)


def norm_rows(slots, mine, twin, gain):
    shape = mine.shape
    return pl.pallas_call(
        functools.partial(norm_kernel, slots, shape[1] * PARTS),
        out_shape=[jax.ShapeDtypeStruct(shape, f32), jax.ShapeDtypeStruct(shape, bf16)],
        in_specs=vmem(3),
        out_specs=vmem(2),
        compiler_params=params(4),
        name="norm_rows",
    )(mine, twin, gain)


def ffn_kernel(n_dp, slots, *refs):
    half = n_dp // 2
    normed_ref = refs[0]
    own, other = refs[1 : 1 + half], refs[1 + half : 1 + n_dp]
    gate_ref, up_ref, down_ref, move_ref, keep_ref, give_ref, units_ref, rows_ref = refs[1 + n_dp :]
    rows = n_dp * slots
    unit, part = normed_ref.shape
    me_head = lax.axis_index("head")
    for s in range(half):
        mine, twins = own[s][...], other[s][...]
        if s == 0:
            mine = jnp.where(me_head == 0, normed_ref[...], mine)
            twins = jnp.where(me_head == 0, twins, normed_ref[...])
        units_ref[pl.ds(s * unit, unit), :] = mine
        units_ref[pl.ds((half + s) * unit, unit), :] = twins
    moved = move_rows(move_ref[...], units_ref[...])
    for q in range(PARTS):
        rows_ref[:, pl.ds(q * part, part)] = moved[q * rows : (q + 1) * rows]
    x = rows_ref[...]
    contract = (((1,), (1,)), ((), ()))
    gate = up = None
    for q in range(PARTS):
        at = pl.ds(q * part, part)
        gate_q = lax.dot_general(x[:, q * part : (q + 1) * part], gate_ref[:, at], contract, preferred_element_type=f32)
        up_q = lax.dot_general(x[:, q * part : (q + 1) * part], up_ref[:, at], contract, preferred_element_type=f32)
        gate = gate_q if q == 0 else gate + gate_q
        up = up_q if q == 0 else up + up_q
    hidden = (gate / (1.0 + jnp.exp(-gate)) * up).astype(bf16)
    write_parts(hidden, lambda q: down_ref[:, pl.ds(q * part, part)], keep_ref, give_ref)


def feed_forward(n_dp, slots, normed, own, other, gate_t, up_t, down, move):
    _, part = normed.shape
    rows = n_dp * slots
    out = lambda dtype: jax.ShapeDtypeStruct((rows * PARTS // 2, part), dtype)
    return pl.pallas_call(
        functools.partial(ffn_kernel, n_dp, slots),
        out_shape=[out(f32), out(bf16)],
        in_specs=vmem(1 + n_dp + 4),
        out_specs=vmem(2),
        scratch_shapes=[VMEM((rows * PARTS, part), bf16), VMEM((rows, PARTS * part), bf16)],
        compiler_params=params(unit_mib(rows, part)),
        name="feed_forward",
    )(normed, *own, *other, gate_t, up_t, down, move)


def final_kernel(slots, owner_rows, live_ref, mine_ref, twin_ref, out_ref):
    me_head = lax.axis_index("head")
    total = mine_ref[...] + twin_ref[...]
    rows = total.shape[0]
    total = jnp.where(live_ref[:, :1] > 0.5, total, 0.0).astype(bf16)
    part = total.shape[1]
    padded = 8
    i = lax.broadcasted_iota(jnp.int32, (padded, rows), 0)
    j = lax.broadcasted_iota(jnp.int32, (padded, rows), 1)
    for q in range(PARTS):
        pick = (j == q * slots + me_head * owner_rows + i).astype(bf16)
        chosen = jnp.dot(pick, total, preferred_element_type=f32)
        out_ref[:, pl.ds(q * part, part)] = chosen[:owner_rows].astype(bf16)


def final_rows(slots, owner_rows, live, mine, twin):
    return pl.pallas_call(
        functools.partial(final_kernel, slots, owner_rows),
        out_shape=jax.ShapeDtypeStruct((owner_rows, mine.shape[1] * PARTS), bf16),
        in_specs=vmem(3),
        out_specs=vmem(1)[0],
        compiler_params=params(4),
        name="final_rows",
    )(live, mine, twin)


def on_device(n_dp, queries, latent_key_cache, lengths, counts, residual, value_up_weight,
              output_proj, norm_gain, gate_weight, up_weight, down_weight):
    slots = queries.shape[0]
    owner_rows = residual.shape[0]
    half = n_dp // 2

    def to_peer(x, k):
        return lax.ppermute(x, "dp", [(i, i ^ k) for i in range(n_dp)])

    def to_twin(x):
        return lax.ppermute(x, "head", [(0, 1), (1, 0)])

    def to_set(x, s):
        pairs = [(2 * i + h, 2 * (i ^ (2 * s + h)) + h) for i in range(n_dp) for h in range(2) if 2 * s + h]
        return lax.ppermute(x, ("dp", "head"), pairs)

    outs = attend(
        n_dp, counts, lengths, queries, latent_key_cache, residual, norm_gain, value_up_weight[0], output_proj[0]
    )
    blocks, (residual_unit, gain_unit, live, to_heads, to_units, to_parts, value_up, most) = outs[:n_dp], outs[n_dp:]
    def reduce_units(keep, give, base, weights):
        units = add_halves(half, keep, to_twin(give), to_units)
        weights = [load(units[0], w) for w in weights]
        got = [to_set(units[s], s) for s in set_order(half)]
        mine = sum_units(units[0], base, got, weights)
        return mine, to_twin(mine), weights

    gate = load(blocks[0], gate_weight.T)
    blocks = [to_peer(blocks[k], k) if k else blocks[0] for k in block_order(n_dp)]
    keep, give = project(n_dp, blocks, value_up, most, to_heads, output_proj[0], gate)
    mine, twin, (up,) = reduce_units(keep, give, residual_unit, [up_weight.T])
    state, normed = norm_rows(slots, mine, twin, gain_unit)
    down = load(normed, down_weight)
    own = {s: to_set(normed, s) for s in reversed(set_order(half))}
    tied = set_order(half)[1]
    own[tied], down = lax.optimization_barrier((own[tied], down))
    other = {s: to_twin(own[s]) for s in set_order(half)}
    own, other = [own[s] for s in range(half)], [other[s] for s in range(half)]
    keep, give = feed_forward(n_dp, slots, normed, own, other, gate, up, down, to_parts)
    mine, twin, _ = reduce_units(keep, give, state, [])
    return final_rows(slots, owner_rows, live, mine, twin)


def solution(mesh):
    n_dp = mesh.shape["dp"]
    in_specs = (
        P(("groups", "dp"), "head", None),
        P(("groups", "dp"), None, None),
        P(("groups", "dp")),
        P("groups"),
        P(("groups", "dp", "head"), None),
        P("head", "dp", None, None),
        P("head", "dp", None),
        P(),
        P(None, ("dp", "head")),
        P(None, ("dp", "head")),
        P(("dp", "head"), None),
    )
    out_specs = P(("groups", "dp", "head"), None)

    def step(*args):
        return on_device(n_dp, *args)

    return jax.shard_map(step, mesh=mesh, in_specs=in_specs, out_specs=out_specs, check_vma=False)
```

```python
import functools

import jax
import jax.numpy as jnp
from jax import lax
from jax.experimental import pallas as pl
from jax.experimental.pallas import tpu as pltpu
from jax.sharding import PartitionSpec as P

LATENT_WIDTH = 512
PIECES = 8
PARTS = 4

score_scale = 0.07216878364870322
norm_epsilon = 1e-06
masked_score = -1e30
f32 = jnp.float32
bf16 = jnp.bfloat16
VMEM = pltpu.VMEM
MIB = 1 << 20


def in_hbm(arrays):
    return [pltpu.with_memory_space_constraint(x, pltpu.HBM) for x in arrays]


def vmem(n):
    return [pl.BlockSpec(memory_space=VMEM)] * n


def params(mib):
    return pltpu.CompilerParams(vmem_limit_bytes=mib * MIB)


def piece_count(rows, most):
    return next(p for p in range(most, 0, -1) if p == 1 or rows % (8 * p) == 0)


def piece_copies(source, target, sems):
    count = sems.shape[0]
    if len(source.shape) == 2:
        count = piece_count(source.shape[0], count)
    step = source.shape[0] // count
    copies = []
    for p in range(count):
        at = pl.ds(p * step, step)
        here = source.at[at]
        if target.shape != source.shape:
            here = source.at[at, pl.ds(0, target.shape[1])]
        copies.append(pltpu.make_async_copy(here, target.at[at], sems.at[p]))
    return copies


def load_kernel(_, source, target, sems):
    copies = piece_copies(source, target, sems)
    for copy in copies:
        copy.start()
    for copy in copies:
        copy.wait()


def load(after, weight):
    return pl.pallas_call(
        load_kernel,
        out_shape=jax.ShapeDtypeStruct(weight.shape, weight.dtype),
        in_specs=[pl.BlockSpec(memory_space=pl.ANY)] * 2,
        out_specs=vmem(1)[0],
        scratch_shapes=[pltpu.SemaphoreType.DMA((PIECES,))],
        compiler_params=params(2),
        cost_estimate=pl.CostEstimate(flops=0, bytes_accessed=4 * weight.size, transcendentals=0),
        name="load",
    )(after, *in_hbm([weight]))


def row_ids(rows, columns, slots):
    i = lax.broadcasted_iota(jnp.int32, (rows, columns), 0).astype(f32)
    unit = float(slots * PARTS)
    block = jnp.floor((i + 0.5) / unit)
    inner = i - block * unit
    part = jnp.floor((inner + 0.5) / slots)
    return part, block * slots + (inner - part * slots)


def attention_kernel(n_dp, counts_hbm, lengths_hbm, q_hbm, cache_hbm, residual_hbm, gain_hbm, *refs):
    n_weights = 2
    weights, outs = refs[:n_weights], refs[n_weights : n_weights + n_dp]
    residual_unit, gain_unit, live_ref, to_heads, to_units, to_parts = refs[n_weights + n_dp : n_weights + n_dp + 6]
    loaded = refs[n_weights + n_dp + 6 : 2 * n_weights + n_dp + 6]
    counts_ref, lengths_ref, q_ref, cache_ref, residual_ref, gain_ref, held, sems, weight_sems = refs[
        2 * n_weights + n_dp + 6 :
    ]
    slots = q_ref.shape[0]
    pairs = [
        (counts_hbm, counts_ref),
        (lengths_hbm, lengths_ref),
        (q_hbm, q_ref),
        (cache_hbm, cache_ref),
        (residual_hbm, residual_ref),
        (gain_hbm, gain_ref),
    ]
    copies = [pltpu.make_async_copy(src, dst, sems.at[n]) for n, (src, dst) in enumerate(pairs)]
    fetches = []
    for n in range(n_weights):
        fetches += piece_copies(weights[n], loaded[n], weight_sems.at[n])
    for copy in copies + fetches:
        copy.start()
    me, me_head = lax.axis_index("dp"), lax.axis_index("head")
    for copy in copies:
        copy.wait()
    rows = range(slots)
    scores = []
    for row in rows:
        score = lax.dot_general(q_ref[row], cache_ref[row], (((1,), (1,)), ((), ())), preferred_element_type=f32)
        position = lax.broadcasted_iota(jnp.int32, score.shape, 1)
        scores.append(jnp.where(position < lengths_ref[row], score * score_scale, masked_score))
    probs = [jnp.exp(x - jnp.max(x, axis=-1, keepdims=True)) for x in scores]
    for row in rows:
        weighted = jnp.dot(probs[row].astype(bf16), cache_ref[row, :, :LATENT_WIDTH], preferred_element_type=f32)
        denominator = jnp.sum(probs[row], axis=-1, keepdims=True)
        latent = jnp.where(row < counts_ref[me], weighted / denominator, 0.0).astype(bf16)
        held[row] = latent.reshape(held.shape[1:])
    for k in range(n_dp):
        for row in rows:
            outs[k][row] = held[row, me ^ k]
    _, slot = row_ids(*live_ref.shape, slots)
    live_ref[...] = (slot < counts_ref[me].astype(f32)).astype(f32)
    to_heads[...] = regroup(to_heads.shape[0], held.shape[2], n_dp * slots)
    to_units[...] = regroup(to_units.shape[0], n_dp // 2, PARTS)
    to_parts[...] = regroup(to_parts.shape[0], PARTS, n_dp)
    owner_rows = residual_ref.shape[0]
    part = residual_unit.shape[1]
    gain = gain_ref[...].reshape(1, PARTS * part)
    residual_unit[...] = jnp.zeros_like(residual_unit)
    for q in range(PARTS):
        at = pl.ds(q * part, part)
        mine = residual_ref[:, at].astype(f32)
        for r in range(owner_rows):
            residual_unit[pl.ds(q * slots + me_head * owner_rows + r, 1), :] = mine[r : r + 1]
        gain_unit[pl.ds(q * slots, slots), :] = jnp.broadcast_to(gain[:, q * part : (q + 1) * part], (slots, part))
    for copy in fetches:
        copy.wait()


def attend(n_dp, counts, lengths, queries, cache, residual, gain, value_up, proj):
    slots, heads, _ = queries.shape
    per_rank = heads // n_dp
    part = gain.shape[0] // PARTS
    block = jax.ShapeDtypeStruct((slots, per_rank, LATENT_WIDTH), bf16)
    unit = jax.ShapeDtypeStruct((slots * PARTS, part), f32)
    rows = n_dp * slots
    live = jax.ShapeDtypeStruct((slots * PARTS, 128), f32)
    moves = [jax.ShapeDtypeStruct((n, n), bf16) for n in (rows * per_rank, rows * PARTS // 2, rows * PARTS)]
    loaded = [
        jax.ShapeDtypeStruct(value_up.shape, bf16),
        jax.ShapeDtypeStruct((proj.shape[0], part * (PARTS - 1)), bf16),
    ]
    return pl.pallas_call(
        functools.partial(attention_kernel, n_dp),
        out_shape=[block] * n_dp + [unit] * 2 + [live] + moves + loaded,
        in_specs=[pl.BlockSpec(memory_space=pl.ANY)] * 8,
        out_specs=vmem(n_dp + 8),
        scratch_shapes=[
            pltpu.SMEM(counts.shape, jnp.int32),
            pltpu.SMEM(lengths.shape, jnp.int32),
            VMEM(queries.shape, bf16),
            VMEM(cache.shape, bf16),
            VMEM(residual.shape, bf16),
            VMEM(gain.shape, f32),
            VMEM((slots, n_dp, per_rank, LATENT_WIDTH), bf16),
            pltpu.SemaphoreType.DMA((6,)),
            pltpu.SemaphoreType.DMA((2, 2)),
        ],
        compiler_params=params(10),
        name="attend",
    )(*in_hbm([counts, lengths, queries, cache, residual, gain, value_up, proj]))


def write_parts(x, weight_part, keep_ref, give_ref):
    half = x.shape[0] // 2
    for q in range(PARTS):
        product = jnp.dot(x, weight_part(q), preferred_element_type=f32)
        at = pl.ds(q * half, half)
        keep_ref[at, :] = product[:half]
        give_ref[at, :] = product[half:].astype(bf16)


def regroup(rows, inner, outer):
    slots = rows // (inner * outer)
    i = lax.broadcasted_iota(jnp.int32, (rows, rows), 0).astype(f32)
    j = lax.broadcasted_iota(jnp.int32, (rows, rows), 1).astype(f32)
    b = jnp.floor((i + 0.5) / (outer * slots))
    rest = i - b * (outer * slots)
    a = jnp.floor((rest + 0.5) / slots)
    return (a * (inner * slots) + b * slots + (rest - a * slots) == j).astype(bf16)


def move_rows(matrix, x):
    return jnp.dot(matrix, x, preferred_element_type=f32).astype(bf16)


def block_order(n_dp):
    far = list(range(n_dp // 2, n_dp))
    return [*far[::-1][1::2], *far[::-1][::2], *reversed(range(n_dp // 2))]


def set_order(half):
    return [*reversed(range(half))]


def project_kernel(n_dp, slots, *refs):
    blocks = refs[:n_dp]
    up_ref, weight_ref, move_ref, weight_hbm, _, keep_ref, give_ref, last_ref, rows_ref, values_ref, sems = refs[n_dp:]
    per_rank = up_ref.shape[0]
    rows = n_dp * slots
    width = last_ref.shape[1]
    copies = piece_copies(weight_hbm.at[:, pl.ds((PARTS - 1) * width, width)], last_ref, sems)
    for copy in copies:
        copy.start()
    me_head = lax.axis_index("head")
    size = slots * per_rank
    for n, k in enumerate(block_order(n_dp)):
        place = ((k & 1) ^ me_head) * (n_dp // 2) + (k >> 1)
        x = blocks[n][...].reshape(size, -1)
        if size % 8 == 0:
            rows_ref[pl.ds(pl.multiple_of(place * size, 8), size), :] = x
        else:
            x = x.astype(f32)
            for c in range(rows_ref.shape[0]):
                rows_ref[c, pl.ds(pl.multiple_of(place * size, 4), size), :] = x[:, c * 128 : (c + 1) * 128]
    if size % 8 == 0:
        gathered = rows_ref[...]
    else:
        gathered = jnp.concatenate([rows_ref[c] for c in range(rows_ref.shape[0])], axis=1).astype(bf16)
    by_head = move_rows(move_ref[...], gathered)
    for j in range(per_rank):
        v = jnp.dot(by_head[j * rows : (j + 1) * rows], up_ref[j], preferred_element_type=f32).astype(bf16)
        values_ref[:, pl.ds(j * v.shape[1], v.shape[1])] = v

    def weight_part(q):
        if q < PARTS - 1:
            return weight_ref[:, pl.ds(q * width, width)]
        for copy in copies:
            copy.wait()
        return last_ref[...]

    write_parts(values_ref[...], weight_part, keep_ref, give_ref)


def unit_mib(rows, part):
    return -(-8 * rows * PARTS * part * 4 // MIB)


def project(n_dp, blocks, value_up, most, move, weight, after):
    slots, per_rank, _ = blocks[0].shape
    depth, width = weight.shape
    rows = n_dp * slots
    part = width // PARTS
    own = rows * PARTS // 2
    out = lambda dtype: jax.ShapeDtypeStruct((own, part), dtype)
    gathered = VMEM((rows * per_rank, LATENT_WIDTH), bf16)
    if slots * per_rank % 8:
        gathered = VMEM((LATENT_WIDTH // 128, rows * per_rank, 128), f32)
    return pl.pallas_call(
        functools.partial(project_kernel, n_dp, slots),
        out_shape=[out(f32), out(bf16)],
        in_specs=vmem(n_dp + 3) + [pl.BlockSpec(memory_space=pl.ANY)] * 2,
        out_specs=vmem(2),
        scratch_shapes=[
            VMEM((depth, part), bf16),
            gathered,
            VMEM((rows, depth), bf16),
            pltpu.SemaphoreType.DMA((PIECES,)),
        ],
        compiler_params=params(unit_mib(rows, part) + 4),
        name="project",
    )(*blocks, value_up, most, move, *in_hbm([weight]), after)


def add_kernel(n_units, keep_ref, got_ref, move_ref, *outs):
    total = (keep_ref[...] + got_ref[...].astype(f32)).astype(bf16)
    units = move_rows(move_ref[...], total)
    size = units.shape[0] // n_units
    for s in range(n_units):
        outs[s][...] = units[s * size : (s + 1) * size]


def add_halves(n_units, keep, got, move):
    unit = keep.shape[0] // n_units
    return pl.pallas_call(
        functools.partial(add_kernel, n_units),
        out_shape=[jax.ShapeDtypeStruct((unit, keep.shape[1]), bf16)] * n_units,
        in_specs=vmem(3),
        out_specs=vmem(n_units),
        compiler_params=params(unit_mib(keep.shape[0] // PARTS, keep.shape[1])),
        name="add_halves",
    )(keep, got, move)


def sum_kernel(n_units, own_ref, base_ref, *refs):
    got, (out_ref, give_ref) = refs[:n_units], refs[-2:]
    me_head = lax.axis_index("head")
    zeroth = set_order(n_units).index(0)
    total = base_ref[...] + jnp.where(me_head == 0, own_ref[...], got[zeroth][...]).astype(f32)
    for ref in got[:zeroth] + got[zeroth + 1 :]:
        total = total + ref[...].astype(f32)
    out_ref[...] = total
    give_ref[...] = total.astype(give_ref.dtype)


def sum_units(own, base, got, after, sent):
    return pl.pallas_call(
        functools.partial(sum_kernel, len(got)),
        out_shape=[jax.ShapeDtypeStruct(own.shape, f32), jax.ShapeDtypeStruct(own.shape, sent)],
        in_specs=vmem(2 + len(got)) + [pl.BlockSpec(memory_space=pl.ANY)] * len(after),
        out_specs=vmem(2),
        compiler_params=params(4),
        name="sum_units",
    )(own, base, *got, *after)


def norm_kernel(slots, width, mine_ref, twin_ref, gain_ref, state_ref, normed_ref):
    state = mine_ref[...] + twin_ref[...]
    square = jnp.sum(state * state, axis=1, keepdims=True)
    rows = state.shape[0]
    _, slot = row_ids(rows, 1, slots)
    first = (lax.axis_index("head") * (slots // 2)).astype(f32)
    owned = (slot >= first) & (slot < first + slots // 2)
    state_ref[...] = jnp.where(owned, state, 0.0)
    mean = jnp.zeros_like(square)
    for r in range(slots):
        total = jnp.sum(jnp.where(slot == r, square, 0.0), axis=0, keepdims=True)
        mean = jnp.where(slot == r, total, mean)
    scaled = state * lax.rsqrt(mean * (1.0 / width) + norm_epsilon)
    normed_ref[...] = (scaled * gain_ref[...]).astype(bf16)


def norm_rows(slots, mine, twin, gain):
    shape = mine.shape
    return pl.pallas_call(
        functools.partial(norm_kernel, slots, shape[1] * PARTS),
        out_shape=[jax.ShapeDtypeStruct(shape, f32), jax.ShapeDtypeStruct(shape, bf16)],
        in_specs=vmem(3),
        out_specs=vmem(2),
        compiler_params=params(4),
        name="norm_rows",
    )(mine, twin, gain)


def ffn_kernel(n_dp, slots, *refs):
    half = n_dp // 2
    normed_ref = refs[0]
    own, other = refs[1 : 1 + half], refs[1 + half : 1 + n_dp]
    gate_ref, up_ref, down_ref, move_ref, keep_ref, give_ref, units_ref, rows_ref = refs[1 + n_dp :]
    rows = n_dp * slots
    unit, part = normed_ref.shape
    me_head = lax.axis_index("head")
    for s in range(half):
        mine, twins = own[s][...], other[s][...]
        if s == 0:
            mine = jnp.where(me_head == 0, normed_ref[...], mine)
            twins = jnp.where(me_head == 0, twins, normed_ref[...])
        units_ref[pl.ds(s * unit, unit), :] = mine
        units_ref[pl.ds((half + s) * unit, unit), :] = twins
    moved = move_rows(move_ref[...], units_ref[...])
    for q in range(PARTS):
        rows_ref[:, pl.ds(q * part, part)] = moved[q * rows : (q + 1) * rows]
    x = rows_ref[...]
    contract = (((1,), (1,)), ((), ()))
    gate = up = None
    for q in range(PARTS):
        at = pl.ds(q * part, part)
        gate_q = lax.dot_general(x[:, q * part : (q + 1) * part], gate_ref[:, at], contract, preferred_element_type=f32)
        up_q = lax.dot_general(x[:, q * part : (q + 1) * part], up_ref[:, at], contract, preferred_element_type=f32)
        gate = gate_q if q == 0 else gate + gate_q
        up = up_q if q == 0 else up + up_q
    hidden = (gate / (1.0 + jnp.exp(-gate)) * up).astype(bf16)
    write_parts(hidden, lambda q: down_ref[:, pl.ds(q * part, part)], keep_ref, give_ref)


def feed_forward(n_dp, slots, normed, own, other, gate_t, up_t, down, move):
    _, part = normed.shape
    rows = n_dp * slots
    out = lambda dtype: jax.ShapeDtypeStruct((rows * PARTS // 2, part), dtype)
    return pl.pallas_call(
        functools.partial(ffn_kernel, n_dp, slots),
        out_shape=[out(f32), out(bf16)],
        in_specs=vmem(1 + n_dp + 4),
        out_specs=vmem(2),
        scratch_shapes=[VMEM((rows * PARTS, part), bf16), VMEM((rows, PARTS * part), bf16)],
        compiler_params=params(unit_mib(rows, part)),
        name="feed_forward",
    )(normed, *own, *other, gate_t, up_t, down, move)


def final_kernel(slots, owner_rows, live_ref, mine_ref, twin_ref, out_ref):
    me_head = lax.axis_index("head")
    total = mine_ref[...] + twin_ref[...].astype(f32)
    rows = total.shape[0]
    total = jnp.where(live_ref[:, :1] > 0.5, total, 0.0).astype(bf16)
    part = total.shape[1]
    padded = 8
    i = lax.broadcasted_iota(jnp.int32, (padded, rows), 0)
    j = lax.broadcasted_iota(jnp.int32, (padded, rows), 1)
    for q in range(PARTS):
        pick = (j == q * slots + me_head * owner_rows + i).astype(bf16)
        chosen = jnp.dot(pick, total, preferred_element_type=f32)
        out_ref[:, pl.ds(q * part, part)] = chosen[:owner_rows].astype(bf16)


def final_rows(slots, owner_rows, live, mine, twin):
    return pl.pallas_call(
        functools.partial(final_kernel, slots, owner_rows),
        out_shape=jax.ShapeDtypeStruct((owner_rows, mine.shape[1] * PARTS), bf16),
        in_specs=vmem(3),
        out_specs=vmem(1)[0],
        compiler_params=params(4),
        name="final_rows",
    )(live, mine, twin)


def on_device(n_dp, queries, latent_key_cache, lengths, counts, residual, value_up_weight,
              output_proj, norm_gain, gate_weight, up_weight, down_weight):
    slots = queries.shape[0]
    owner_rows = residual.shape[0]
    half = n_dp // 2

    def to_peer(x, k):
        return lax.ppermute(x, "dp", [(i, i ^ k) for i in range(n_dp)])

    def to_twin(x):
        return lax.ppermute(x, "head", [(0, 1), (1, 0)])

    def to_set(x, s):
        pairs = [(2 * i + h, 2 * (i ^ (2 * s + h)) + h) for i in range(n_dp) for h in range(2) if 2 * s + h]
        return lax.ppermute(x, ("dp", "head"), pairs)

    outs = attend(
        n_dp, counts, lengths, queries, latent_key_cache, residual, norm_gain, value_up_weight[0], output_proj[0]
    )
    blocks, (residual_unit, gain_unit, live, to_heads, to_units, to_parts, value_up, most) = outs[:n_dp], outs[n_dp:]
    def reduce_units(keep, give, base, weights):
        units = add_halves(half, keep, to_twin(give), to_units)
        weights = [load(units[0], w) for w in weights]
        got = [to_set(units[s], s) for s in set_order(half)]
        mine, give = sum_units(units[0], base, got, weights, f32 if weights else bf16)
        return mine, to_twin(give), weights

    gate = load(blocks[0], gate_weight.T)
    blocks = [to_peer(blocks[k], k) if k else blocks[0] for k in block_order(n_dp)]
    keep, give = project(n_dp, blocks, value_up, most, to_heads, output_proj[0], gate)
    mine, twin, (up,) = reduce_units(keep, give, residual_unit, [up_weight.T])
    state, normed = norm_rows(slots, mine, twin, gain_unit)
    down = load(normed, down_weight)
    own = {s: to_set(normed, s) for s in reversed(set_order(half))}
    tied = set_order(half)[1]
    own[tied], down = lax.optimization_barrier((own[tied], down))
    other = {s: to_twin(own[s]) for s in set_order(half)}
    own, other = [own[s] for s in range(half)], [other[s] for s in range(half)]
    keep, give = feed_forward(n_dp, slots, normed, own, other, gate, up, down, to_parts)
    mine, twin, _ = reduce_units(keep, give, state, [])
    return final_rows(slots, owner_rows, live, mine, twin)


def solution(mesh):
    n_dp = mesh.shape["dp"]
    in_specs = (
        P(("groups", "dp"), "head", None),
        P(("groups", "dp"), None, None),
        P(("groups", "dp")),
        P("groups"),
        P(("groups", "dp", "head"), None),
        P("head", "dp", None, None),
        P("head", "dp", None),
        P(),
        P(None, ("dp", "head")),
        P(None, ("dp", "head")),
        P(("dp", "head"), None),
    )
    out_specs = P(("groups", "dp", "head"), None)

    def step(*args):
        return on_device(n_dp, *args)

    return jax.shard_map(step, mesh=mesh, in_specs=in_specs, out_specs=out_specs, check_vma=False)
```
